128 devices in a mesh: chan: 16 (over z, x_hi, core), win: 8 (over y, x_lo).
Axes of the slice: x: 4 (x_hi: 2, x_lo: 2; x = x_hi * 2 + x_lo), y: 4, z: 4, core: 2. Of those that a mesh axis runs over, the one named last changes fastest.
Arguments:
- series: bfloat16 [64, 2048, 1500], P('win', 'chan'), may hold values from -1700 to 1700
- validity: int32 [64, 2048], P('win', 'chan'), may hold values from 0 to 1, as said below
Outputs:
- source_gathers: float32 [2048, 16, 8, 16, 128], P('chan', None, 'win')
The draws below stay inside these ranges and needn't reach their ends.
Inputs may be any that keep to these rules, and one draw needn't show every extreme that they name: `validity`: a channel flagged dead is 0 in every window.
All inputs are finite; a program needn't handle non-finite values.
Results may differ from the reference program's by a relative error of at most 0.0037.
Values may be sent and summed in bfloat16 or wider, within the bound.
No kernel may reach another device: no remote copies, remote signals or barrier semaphores. Data moves between devices by JAX's collectives and lax.ppermute only.
A program may use at most 192 MiB of HBM per device.

```python
import math
import jax
import jax.numpy as jnp
from jax import lax

CHANNELS = 2048
SAMPLES = 1500
BINS = 128
LAGS = 128
SOURCES = 2048
WINDOWS = 64
CH_SUB = 16
N_CHAN = 16
N_WIN = 8


def draw_series(key, part):
    subkeys = jax.random.split(key, 3)
    full_shape = (WINDOWS, CHANNELS, SAMPLES)
    noise_base = jnp.clip(jax.random.normal(subkeys[0], full_shape, jnp.float32), -6.0, 6.0)
    log_top = math.log(10.0)
    chan_scale = jnp.exp(jax.random.uniform(subkeys[1], (1, CHANNELS, 1), jnp.float32, 0.0, log_top))
    window_scale = jnp.exp(jax.random.uniform(subkeys[2], (WINDOWS, 1, 1), jnp.float32, 0.0, log_top))
    return (noise_base * chan_scale * window_scale).astype(jnp.bfloat16)


def draw_validity(key, part):
    subkeys = jax.random.split(key, 2)
    dead_channel = jax.random.randint(subkeys[0], (1, CHANNELS), 0, 16) == 0
    glitch = jax.random.randint(subkeys[1], (WINDOWS, CHANNELS), 0, 100) < 15
    return jnp.where(dead_channel | glitch, 0, 1).astype(jnp.int32)


def setup_inputs(seed: int = 0) -> dict:
    keys = jax.random.split(jax.random.key(seed), 3)
    return {
        "series": draw_series(jax.random.fold_in(keys[2], 71), 0),
        "validity": draw_validity(jax.random.fold_in(keys[2], 71), 0),
    }


lowest_bin = 6

def build_tables():
    sample_idx = jnp.arange(SAMPLES, dtype=jnp.int32)
    bin_idx = jnp.arange(BINS, dtype=jnp.int32) + lowest_bin
    phase_index = sample_idx[:, None] * bin_idx[None, :] % SAMPLES
    phase_angle = phase_index.astype(jnp.float32) * (2.0 * math.pi / SAMPLES)
    hann_taper = 0.5 - 0.5 * jnp.cos(sample_idx.astype(jnp.float32) * (2.0 * math.pi / SAMPLES))
    taper_table = jnp.concatenate([hann_taper[:, None] * jnp.cos(phase_angle), -hann_taper[:, None] * jnp.sin(phase_angle)], axis=1).astype(jnp.bfloat16)
    lag_idx = jnp.arange(LAGS, dtype=jnp.int32) - LAGS // 2
    lag_index = bin_idx[:, None] * lag_idx[None, :] % SAMPLES
    lag_angle = lag_index.astype(jnp.float32) * (2.0 * math.pi / SAMPLES)
    inverse = jnp.concatenate([jnp.cos(lag_angle), -jnp.sin(lag_angle)], axis=0)
    return (taper_table, inverse)

def reference(series, validity):
    taper_table, inverse = build_tables()
    stride = CHANNELS // SOURCES
    flag_float = validity.astype(jnp.float32)
    spectra = jnp.dot(series.reshape(WINDOWS * CHANNELS, SAMPLES), taper_table, preferred_element_type=jnp.float32)
    spectra = spectra.reshape(WINDOWS, CHANNELS, 2 * BINS)
    energy = lax.optimization_barrier(jnp.mean(spectra * spectra, axis=-1, keepdims=True))
    rounded = (spectra * lax.rsqrt(energy + 1e-06) * flag_float[..., None]).astype(jnp.bfloat16)
    whitened = lax.optimization_barrier(rounded).astype(jnp.float32)
    recv_real = whitened[..., :BINS]
    recv_imag = whitened[..., BINS:]
    block_size = SOURCES // 16
    sources = whitened[:, ::stride].reshape(WINDOWS, 16, block_size, 2 * BINS).transpose(1, 0, 2, 3)

    def one_block(source_block):
        src_real = source_block[..., :BINS]
        src_imag = source_block[..., BINS:]
        in_phase = jnp.einsum('wsk,wik->sik', src_real, recv_real) + jnp.einsum('wsk,wik->sik', src_imag, recv_imag)
        quadrature = jnp.einsum('wsk,wik->sik', src_real, recv_imag) - jnp.einsum('wsk,wik->sik', src_imag, recv_real)
        joined = jnp.concatenate([in_phase, quadrature], axis=-1)
        return jnp.einsum('sik,kt->sit', joined, inverse, precision=lax.Precision.HIGHEST)
    correlation = lax.map(one_block, sources).reshape(SOURCES, CHANNELS, LAGS)
    pair_count = jnp.einsum('ws,wi->si', flag_float[:, ::stride], flag_float, precision=lax.Precision.HIGHEST)
    result = correlation / jnp.maximum(pair_count, 1.0)[..., None]
    return result.reshape(SOURCES, N_CHAN, N_WIN, CH_SUB, LAGS)
```

```python
import math

import jax
import jax.numpy as jnp
import numpy as np
from jax import lax
from jax.experimental import pallas as pl
from jax.experimental.pallas import tpu as pltpu
from jax.sharding import PartitionSpec as P

SAMPLES = 1500
BINS = 128
LAGS = 128
LOWEST = 6
ROWS = BINS + 1
CHUNK = 43
STEPS = ROWS // CHUNK
PITCH = 2 * BINS + 8
VMEM_LIMIT = 60 << 20


def build_tables():
    t = np.arange(SAMPLES)
    k = np.arange(BINS) + LOWEST
    angle = ((t[:, None] * k[None, :]) % SAMPLES).astype(np.float32) * np.float32(2.0 * math.pi / SAMPLES)
    hann = np.float32(0.5) - np.float32(0.5) * np.cos(t.astype(np.float32) * np.float32(2.0 * math.pi / SAMPLES))
    taper = np.concatenate([hann[:, None] * np.cos(angle), -hann[:, None] * np.sin(angle)], axis=1)
    taper = np.ascontiguousarray(taper.T).astype(jnp.bfloat16)
    j = np.arange(LAGS) - LAGS // 2
    lag_angle = ((k[:, None] * j[None, :]) % SAMPLES).astype(np.float32) * np.float32(2.0 * math.pi / SAMPLES)
    inverse = np.concatenate([np.cos(lag_angle), -np.sin(lag_angle)], axis=0)
    inverse = np.ascontiguousarray(inverse.T).astype(np.float32)
    high = inverse.astype(jnp.bfloat16)
    low = (inverse - high.astype(np.float32)).astype(jnp.bfloat16)
    return taper, high, low


def spectra_call(series, validity, taper):
    windows, channels, _ = series.shape
    slots = channels // 16
    groups = BINS // 8 + 1

    def kernel(x_ref, v_ref, t_ref, w_ref, p_ref, scr):
        g = pl.program_id(0)
        x = x_ref[...].reshape(2 * channels, SAMPLES)
        s = lax.dot_general(t_ref[...], x, (((1,), (1,)), ((), ())), preferred_element_type=jnp.float32)
        energy = jnp.sum(s * s, axis=0, keepdims=True) * (1.0 / (2 * BINS))
        flags = v_ref[pl.ds(2 * g, 2), :].astype(jnp.float32)
        flags = jnp.concatenate([flags[0:1], flags[1:2]], axis=1)
        s = s * lax.rsqrt(energy + 1e-06) * flags
        for h in range(2):
            for part in range(2):
                scr[pl.ds(part * 8 + 2 * g + h, BINS, stride=16), :] = s[
                    part * BINS : (part + 1) * BINS, h * channels : (h + 1) * channels
                ]

        @pl.when(g == pl.num_programs(0) - 1)
        def _():
            for b in range(BINS // 8):
                block = scr[b * 128 : (b + 1) * 128, :]
                w_ref[b * 8 : (b + 1) * 8] = block.astype(jnp.bfloat16).reshape(8, 16, channels)
                p_ref[:, b] = block.T.astype(jnp.bfloat16).reshape(slots, 16, 128)
            f = v_ref[...].astype(jnp.float32)
            f = jnp.concatenate([f, jnp.zeros((8, channels), jnp.float32)], axis=0)
            w_ref[BINS] = f.astype(jnp.bfloat16)
            f = jnp.concatenate([f, jnp.zeros((112, channels), jnp.float32)], axis=0)
            p_ref[:, groups - 1] = f.T.astype(jnp.bfloat16).reshape(slots, 16, 128)

    return pl.pallas_call(
        kernel,
        grid=(windows // 2,),
        in_specs=[
            pl.BlockSpec((2, channels, SAMPLES), lambda g: (g, 0, 0)),
            pl.BlockSpec((windows, channels), lambda g: (0, 0)),
            pl.BlockSpec((2 * BINS, SAMPLES), lambda g: (0, 0)),
        ],
        out_specs=[
            pl.BlockSpec((ROWS, 16, channels), lambda g: (0, 0, 0)),
            pl.BlockSpec((slots, groups, 16, 128), lambda g: (0, 0, 0, 0)),
        ],
        out_shape=[
            jax.ShapeDtypeStruct((ROWS, 16, channels), jnp.bfloat16),
            jax.ShapeDtypeStruct((slots, groups, 16, 128), jnp.bfloat16),
        ],
        scratch_shapes=[pltpu.VMEM((BINS * 16, channels), jnp.float32)],
        compiler_params=pltpu.CompilerParams(dimension_semantics=("arbitrary",), vmem_limit_bytes=VMEM_LIMIT),
        name="spectra",
    )(series, validity, taper)


def slot_call(order, parts):
    count, groups = parts.shape[:2]

    def kernel(order_ref, p_ref, r_ref):
        def rows(b, places):
            return [p_ref[order_ref[q], b] for q in range(count)]

        def body(b, _):
            tiles = rows(b, count)
            for e in range(8):
                r_ref[b * 8 + e] = jnp.concatenate([t[:, 16 * e : 16 * e + 16] for t in tiles], axis=1)
            return 0

        lax.fori_loop(0, groups - 1, body, 0, unroll=4)
        r_ref[BINS] = jnp.concatenate([t[:, :16] for t in rows(groups - 1, count)], axis=1)

    return pl.pallas_call(
        kernel,
        grid_spec=pltpu.PrefetchScalarGridSpec(
            num_scalar_prefetch=1,
            grid=(1,),
            in_specs=[pl.BlockSpec(parts.shape, lambda g, o: (0, 0, 0, 0))],
            out_specs=pl.BlockSpec((ROWS, 16, 128), lambda g, o: (0, 0, 0)),
        ),
        out_shape=jax.ShapeDtypeStruct((ROWS, 16, 128), jnp.bfloat16),
        compiler_params=pltpu.CompilerParams(dimension_semantics=("arbitrary",), vmem_limit_bytes=VMEM_LIMIT),
        name="slot",
    )(order, parts)


def pair_call(places, sources, receivers, high, low, blocks, previous=None):
    count = len(receivers)
    rows = 16 * count

    def kernel(place_ref, *refs):
        del place_ref
        src = refs[:8]
        rcv = refs[8 : 8 + count]
        hi_ref, lo_ref = refs[8 + count : 10 + count]
        out, joined, recip = refs[-3:]
        g = pl.program_id(0)

        def one_bin(k):
            tiles = [s[k] for s in src]
            swapped = []
            for tile in tiles:
                f = tile.astype(jnp.float32)
                swapped.append(jnp.concatenate([-f[8:], f[:8]], axis=0).astype(jnp.bfloat16))
            weights = jnp.concatenate([jnp.concatenate(tiles, axis=0), jnp.concatenate(swapped, axis=0)], axis=1)
            lhs = jnp.concatenate([r[k] for r in rcv], axis=0)
            return jnp.dot(lhs, weights, preferred_element_type=jnp.float32)

        def store_bin(k, _):
            both = one_bin(k)
            at = g * CHUNK + k
            joined[pl.ds(at, rows, stride=PITCH), :] = both[:, :128]
            joined[pl.ds(at + BINS, rows, stride=PITCH), :] = both[:, 128:]
            return 0

        @pl.when(g < STEPS)
        def _():
            lax.fori_loop(0, CHUNK - 1, store_bin, 0, unroll=14)

        @pl.when(g < STEPS - 1)
        def _():
            store_bin(CHUNK - 1, 0)

        @pl.when(g == STEPS - 1)
        def _():
            recip[...] = 1.0 / jnp.maximum(one_bin(CHUNK - 1)[:, :128], 1.0)

        @pl.when(g >= STEPS)
        def _():
            flat = out.reshape(2048, LAGS)

            def body(q, _):
                i = (g - STEPS) * 16 + 2 * q
                first = pl.multiple_of(i * PITCH, 8)
                second = pl.multiple_of((i + 1) * PITCH, 8)
                pair = jnp.concatenate([joined[pl.ds(first, 256), :], joined[pl.ds(second, 256), :]], axis=1)
                upper = pair.astype(jnp.bfloat16)
                lower = (pair - upper.astype(jnp.float32)).astype(jnp.bfloat16)
                acc = jnp.dot(hi_ref[...], upper, preferred_element_type=jnp.float32)
                acc = acc + jnp.dot(lo_ref[...], upper, preferred_element_type=jnp.float32)
                acc = acc + jnp.dot(hi_ref[...], lower, preferred_element_type=jnp.float32)
                scale = jnp.concatenate([recip[pl.ds(i, 1), :], recip[pl.ds(i + 1, 1), :]], axis=1)
                acc = acc * scale
                flat[pl.ds(2 * q, 128, stride=16), :] = acc[:, :128].T
                flat[pl.ds(2 * q + 1, 128, stride=16), :] = acc[:, 128:].T
                return 0

            lax.fori_loop(0, 8, body, 0, unroll=8)

    piece = pl.BlockSpec((CHUNK, 16, 128), lambda g, at: (jnp.minimum(g, STEPS - 1), 0, 0))
    table = pl.BlockSpec((LAGS, 2 * BINS), lambda g, at: (0, 0))
    in_specs = [piece] * (8 + count) + [table] * 2
    operands = [*sources, *receivers, high, low]
    aliases = {}
    if previous is not None:
        in_specs.append(pl.BlockSpec(memory_space=pl.ANY))
        aliases = {1 + len(operands): 0}
        operands.append(previous)
    macs = (ROWS * 128 * 256 + 128 * 128 * 256 * 3) * rows
    return pl.pallas_call(
        kernel,
        grid_spec=pltpu.PrefetchScalarGridSpec(
            num_scalar_prefetch=1,
            grid=(STEPS + count,),
            in_specs=in_specs,
            out_specs=pl.BlockSpec(
                (128, 1, 1, 16, LAGS), lambda g, at: (0, at[jnp.maximum(g - STEPS, 0)], 0, 0, 0)
            ),
            scratch_shapes=[pltpu.VMEM((rows * PITCH, 128), jnp.float32), pltpu.VMEM((rows, 128), jnp.float32)],
        ),
        out_shape=jax.ShapeDtypeStruct((128, blocks, 1, 16, LAGS), jnp.float32),
        input_output_aliases=aliases,
        compiler_params=pltpu.CompilerParams(dimension_semantics=("arbitrary",), vmem_limit_bytes=VMEM_LIMIT),
        cost_estimate=pl.CostEstimate(flops=2 * macs, bytes_accessed=(8 + count) * ROWS * 4096, transcendentals=0),
        name=f"pair{count}",
    )(places, *operands)


def solution(mesh):
    taper, high, low = build_tables()

    def chan_of(z, h, c):
        return (z % 4) * 4 + (h % 2) * 2 + c % 2

    def win_of(y, x):
        return (y % 4) * 2 + x % 2

    def over_chan(a, dz=0, dh=0, dc=0):
        perm = [(chan_of(z, h, c), chan_of(z + dz, h + dh, c + dc)) for z in range(4) for h in range(2) for c in range(2)]
        return lax.ppermute(a, "chan", perm)

    def over_win(a, dy=0, dx=0):
        perm = [(win_of(y, x), win_of(y + dy, x + dx)) for y in range(4) for x in range(2)]
        return lax.ppermute(a, "win", perm)

    ring_order = ((0, 0), (0, 1), (-1, 0), (1, 0), (-1, 1), (1, 1), (-2, 0), (2, 1))

    def on_device(series, validity):
        own, slots = spectra_call(series, validity, taper)

        side = over_win(own, dx=1)
        up, down = over_win(own, dy=1), over_win(own, dy=-1)
        side_up, side_down = over_win(side, dy=1), over_win(side, dy=-1)
        sources = [own, side, up, down, side_up, side_down, over_win(up, dy=1), over_win(side_down, dy=-1)]

        parts = lax.all_to_all(slots, "win", split_axis=0, concat_axis=0, tiled=True)
        w = lax.axis_index("win")
        y, x = w // 2, w % 2
        order = jnp.stack([((y + dy) % 4) * 2 + (x + dx) % 2 for dy, dx in ring_order]).astype(jnp.int32)
        mine = slot_call(order, parts)
        side = over_chan(mine, dh=1)
        up, down = over_chan(mine, dz=1), over_chan(mine, dz=-1)
        side_up, side_down = over_chan(side, dz=1), over_chan(side, dz=-1)
        receivers = [mine, side, up, down, side_up, side_down, over_chan(up, dz=1), over_chan(side_down, dz=-1)]
        receivers = receivers + [over_chan(r, dc=1) for r in receivers]
        ch = lax.axis_index("chan")
        z, h, c = ch // 4, (ch // 2) % 2, ch % 2
        places = jnp.stack(
            [((z + dz) % 4) * 4 + ((h + dh) % 2) * 2 + (c + dc) % 2 for dc in range(2) for dz, dh in ring_order]
        ).astype(jnp.int32)
        return pair_call(places, sources, receivers, high, low, 16)

    return jax.shard_map(
        on_device,
        mesh=mesh,
        in_specs=(P("win", "chan", None), P("win", "chan")),
        out_specs=P("chan", None, "win", None, None),
        check_vma=False,
    )
```

```python
import math

import jax
import jax.numpy as jnp
import numpy as np
from jax import lax
from jax.experimental import pallas as pl
from jax.experimental.pallas import tpu as pltpu
from jax.sharding import PartitionSpec as P

SAMPLES = 1500
BINS = 128
LAGS = 128
LOWEST = 6
ROWS = BINS + 1
CHUNK = 43
STEPS = ROWS // CHUNK
PITCH = 2 * BINS + 8
ROW = 24
SPAN = 512
VMEM_LIMIT = 60 << 20


def build_tables():
    t = np.arange(SAMPLES)
    k = np.arange(BINS) + LOWEST
    angle = ((t[:, None] * k[None, :]) % SAMPLES).astype(np.float32) * np.float32(2.0 * math.pi / SAMPLES)
    hann = np.float32(0.5) - np.float32(0.5) * np.cos(t.astype(np.float32) * np.float32(2.0 * math.pi / SAMPLES))
    taper = np.concatenate([hann[:, None] * np.cos(angle), -hann[:, None] * np.sin(angle)], axis=1)
    taper = np.pad(taper.T, ((0, 0), (0, -SAMPLES % SPAN))).astype(jnp.bfloat16)
    j = np.arange(LAGS) - LAGS // 2
    lag_angle = ((k[:, None] * j[None, :]) % SAMPLES).astype(np.float32) * np.float32(2.0 * math.pi / SAMPLES)
    inverse = np.concatenate([np.cos(lag_angle), -np.sin(lag_angle)], axis=0)
    inverse = np.ascontiguousarray(inverse.T).astype(np.float32)
    high = inverse.astype(jnp.bfloat16)
    low = (inverse - high.astype(np.float32)).astype(jnp.bfloat16)
    return taper, high, low


def spectra_call(series, validity, taper):
    windows, channels, _ = series.shape
    slots = channels // 16
    groups = BINS // 8 + 1
    steps = taper.shape[1] // SPAN
    tail = SAMPLES - (steps - 1) * SPAN
    by_time = jnp.transpose(series, (2, 0, 1))

    def kernel(x_ref, v_ref, t_ref, w_ref, p_ref, turned, acc, scr):
        g = pl.program_id(0)

        def turn(q, _):
            block = x_ref[pl.ds(q * 4, 4)].astype(jnp.float32)
            for e in range(4):
                turned[pl.ds(q * 4 + e, windows, stride=SPAN + 8), :] = block[e]
            return 0

        @pl.when(g == 0)
        def _():
            acc[...] = jnp.zeros_like(acc)

        @pl.when(g < steps - 1)
        def _():
            lax.fori_loop(0, SPAN // 4, turn, 0, unroll=16)

        @pl.when(g == steps - 1)
        def _():
            lax.fori_loop(0, tail // 4, turn, 0, unroll=17)
            for q in range(tail, SPAN):
                turned[pl.ds(q, windows, stride=SPAN + 8), :] = jnp.zeros((windows, channels), jnp.float32)

        for h in range(windows // 2):
            cols = [turned[(2 * h + e) * (SPAN + 8) : (2 * h + e) * (SPAN + 8) + SPAN, :] for e in range(2)]
            cols = jnp.concatenate(cols, axis=1).astype(jnp.bfloat16)
            acc[h] += jnp.dot(t_ref[...], cols, preferred_element_type=jnp.float32)

        @pl.when(g == steps - 1)
        def _():
            for h in range(windows // 2):
                s = acc[h]
                energy = jnp.sum(s * s, axis=0, keepdims=True) * (1.0 / (2 * BINS))
                flags = v_ref[2 * h : 2 * h + 2, :].astype(jnp.float32)
                flags = jnp.concatenate([flags[0:1], flags[1:2]], axis=1)
                s = s * lax.rsqrt(energy + 1e-06) * flags
                for e in range(2):
                    for part in range(2):
                        scr[pl.ds(part * 8 + 2 * h + e, BINS, stride=16), :] = s[
                            part * BINS : (part + 1) * BINS, e * channels : (e + 1) * channels
                        ]
            for b in range(BINS // 8):
                block = scr[b * 128 : (b + 1) * 128, :]
                w_ref[b * 8 : (b + 1) * 8] = block.astype(jnp.bfloat16).reshape(8, 16, channels)
                p_ref[:, b] = block.T.astype(jnp.bfloat16).reshape(slots, 16, 128)
            f = v_ref[...].astype(jnp.float32)
            f = jnp.concatenate([f, jnp.zeros((8, channels), jnp.float32)], axis=0)
            w_ref[BINS] = f.astype(jnp.bfloat16)
            f = jnp.concatenate([f, jnp.zeros((112, channels), jnp.float32)], axis=0)
            p_ref[:, groups - 1] = f.T.astype(jnp.bfloat16).reshape(slots, 16, 128)

    return pl.pallas_call(
        kernel,
        grid=(steps,),
        in_specs=[
            pl.BlockSpec((SPAN, windows, channels), lambda g: (g, 0, 0)),
            pl.BlockSpec((windows, channels), lambda g: (0, 0)),
            pl.BlockSpec((2 * BINS, SPAN), lambda g: (0, g)),
        ],
        out_specs=[
            pl.BlockSpec((ROWS, 16, channels), lambda g: (0, 0, 0)),
            pl.BlockSpec((slots, groups, 16, 128), lambda g: (0, 0, 0, 0)),
        ],
        out_shape=[
            jax.ShapeDtypeStruct((ROWS, 16, channels), jnp.bfloat16),
            jax.ShapeDtypeStruct((slots, groups, 16, 128), jnp.bfloat16),
        ],
        scratch_shapes=[
            pltpu.VMEM((windows * (SPAN + 8), channels), jnp.float32),
            pltpu.VMEM((windows // 2, 2 * BINS, 2 * channels), jnp.float32),
            pltpu.VMEM((BINS * 16, channels), jnp.float32),
        ],
        compiler_params=pltpu.CompilerParams(dimension_semantics=("arbitrary",), vmem_limit_bytes=VMEM_LIMIT),
        name="spectra",
    )(by_time, validity, taper)


def slot_call(order, parts):
    count, groups = parts.shape[:2]

    span = 6
    steps = pl.cdiv(groups, span)
    whole = groups - 1 - (steps - 1) * span

    def kernel(order_ref, p_ref, r_ref):
        g = pl.program_id(0)

        def body(b, _):
            tiles = [p_ref[order_ref[q], b] for q in range(count)]
            for e in range(8):
                r_ref[b * 8 + e] = jnp.concatenate([t[:, 16 * e : 16 * e + 16] for t in tiles], axis=1)
            return 0

        @pl.when(g < steps - 1)
        def _():
            lax.fori_loop(0, span, body, 0, unroll=span)

        @pl.when(g == steps - 1)
        def _():
            lax.fori_loop(0, whole, body, 0, unroll=whole)
            r_ref[whole * 8] = jnp.concatenate([p_ref[order_ref[q], whole][:, :16] for q in range(count)], axis=1)

    return pl.pallas_call(
        kernel,
        grid_spec=pltpu.PrefetchScalarGridSpec(
            num_scalar_prefetch=1,
            grid=(steps,),
            in_specs=[pl.BlockSpec((count, span, 16, 128), lambda g, o: (0, g, 0, 0))],
            out_specs=pl.BlockSpec((span * 8, 16, 128), lambda g, o: (g, 0, 0)),
        ),
        out_shape=jax.ShapeDtypeStruct((ROWS, 16, 128), jnp.bfloat16),
        compiler_params=pltpu.CompilerParams(dimension_semantics=("arbitrary",), vmem_limit_bytes=VMEM_LIMIT),
        name="slot",
    )(order, parts)


def pair_call(places, sources, receivers, high, low, blocks, previous=None):
    count = len(receivers)
    rows = 16 * count

    def kernel(place_ref, *refs):
        src = refs[:8]
        rcv = refs[8 : 8 + count]
        hi_ref, lo_ref = refs[8 + count : 10 + count]
        out, joined, recip, held, sent = refs[-5:]
        g = pl.program_id(0)

        def one_bin(k):
            tiles = [s[k] for s in src]
            swapped = []
            for tile in tiles:
                f = tile.astype(jnp.float32)
                swapped.append(jnp.concatenate([-f[8:], f[:8]], axis=0).astype(jnp.bfloat16))
            weights = jnp.concatenate([jnp.concatenate(tiles, axis=0), jnp.concatenate(swapped, axis=0)], axis=1)
            lhs = jnp.concatenate([r[k] for r in rcv], axis=0)
            return jnp.dot(lhs, weights, preferred_element_type=jnp.float32)

        def store_bin(k, _):
            both = one_bin(k)
            at = g * CHUNK + k
            joined[pl.ds(at, rows, stride=PITCH), :] = both[:, :128]
            joined[pl.ds(at + BINS, rows, stride=PITCH), :] = both[:, 128:]
            return 0

        @pl.when(g < STEPS)
        def _():
            lax.fori_loop(0, CHUNK - 1, store_bin, 0, unroll=42)

        @pl.when(g < STEPS - 1)
        def _():
            store_bin(CHUNK - 1, 0)

        @pl.when(g == STEPS - 1)
        def _():
            recip[...] = 1.0 / jnp.maximum(one_bin(CHUNK - 1)[:, :128], 1.0)

        @pl.when(g >= STEPS)
        def _():
            block = g - STEPS
            slot = lax.rem(block, 2)

            def write(which, at):
                return pltpu.make_async_copy(
                    held.at[at, :, pl.ds(0, 16), :], out.at[:, place_ref[which], 0], sent.at[at]
                )

            @pl.when(block >= 2)
            def _():
                write(block - 2, slot).wait()

            flat = held.at[slot].reshape(128 * ROW, LAGS)

            def body(q, _):
                i = (g - STEPS) * 16 + 2 * q
                first = pl.multiple_of(i * PITCH, 8)
                second = pl.multiple_of((i + 1) * PITCH, 8)
                pair = jnp.concatenate([joined[pl.ds(first, 256), :], joined[pl.ds(second, 256), :]], axis=1)
                upper = pair.astype(jnp.bfloat16)
                lower = (pair - upper.astype(jnp.float32)).astype(jnp.bfloat16)
                tables = jnp.concatenate([hi_ref[...], lo_ref[...]], axis=0)
                acc = jnp.dot(tables, upper, preferred_element_type=jnp.float32)
                acc = acc[:LAGS] + acc[LAGS:] + jnp.dot(hi_ref[...], lower, preferred_element_type=jnp.float32)
                scale = jnp.concatenate([recip[pl.ds(i, 1), :], recip[pl.ds(i + 1, 1), :]], axis=1)
                acc = acc * scale
                flat[pl.ds(2 * q, 128, stride=ROW), :] = acc[:, :128].T
                flat[pl.ds(2 * q + 1, 128, stride=ROW), :] = acc[:, 128:].T
                return 0

            lax.fori_loop(0, 8, body, 0, unroll=8)
            write(block, slot).start()

            @pl.when(block == count - 1)
            def _():
                write(block - 1, 1 - slot).wait()
                write(block, slot).wait()

    piece = pl.BlockSpec((CHUNK, 16, 128), lambda g, at: (jnp.minimum(g, STEPS - 1), 0, 0))
    table = pl.BlockSpec((LAGS, 2 * BINS), lambda g, at: (0, 0))
    in_specs = [piece] * (8 + count) + [table] * 2
    operands = [*sources, *receivers, high, low]
    aliases = {}
    if previous is not None:
        in_specs.append(pl.BlockSpec(memory_space=pl.ANY))
        aliases = {1 + len(operands): 0}
        operands.append(previous)
    macs = (ROWS * 128 * 256 + 128 * 128 * 256 * 3) * rows
    return pl.pallas_call(
        kernel,
        grid_spec=pltpu.PrefetchScalarGridSpec(
            num_scalar_prefetch=1,
            grid=(STEPS + count,),
            in_specs=in_specs,
            out_specs=pl.BlockSpec(memory_space=pl.ANY),
            scratch_shapes=[
                pltpu.VMEM((rows * PITCH, 128), jnp.float32),
                pltpu.VMEM((rows, 128), jnp.float32),
                pltpu.VMEM((2, 128, ROW, LAGS), jnp.float32),
                pltpu.SemaphoreType.DMA((2,)),
            ],
        ),
        out_shape=jax.ShapeDtypeStruct((128, blocks, 1, 16, LAGS), jnp.float32),
        input_output_aliases=aliases,
        compiler_params=pltpu.CompilerParams(dimension_semantics=("arbitrary",), vmem_limit_bytes=VMEM_LIMIT),
        cost_estimate=pl.CostEstimate(flops=2 * macs, bytes_accessed=(8 + count) * ROWS * 4096, transcendentals=0),
    )(places, *operands)


def solution(mesh):
    taper, high, low = build_tables()

    def chan_of(z, h, c):
        return (z % 4) * 4 + (h % 2) * 2 + c % 2

    def win_of(y, x):
        return (y % 4) * 2 + x % 2

    def over_chan(a, dz=0, dh=0, dc=0):
        perm = [(chan_of(z, h, c), chan_of(z + dz, h + dh, c + dc)) for z in range(4) for h in range(2) for c in range(2)]
        return lax.ppermute(a, "chan", perm)

    def over_win(a, dy=0, dx=0):
        perm = [(win_of(y, x), win_of(y + dy, x + dx)) for y in range(4) for x in range(2)]
        return lax.ppermute(a, "win", perm)

    ring_order = ((0, 0), (0, 1), (-1, 0), (1, 0), (-1, 1), (1, 1), (-2, 0), (2, 1))

    def step(move, value, **by):
        return move(value, **by)

    def stages(series, validity):
        own, slots = spectra_call(series, validity, taper)

        parts = lax.all_to_all(slots, "win", split_axis=0, concat_axis=0, tiled=True)
        side = step(over_win, own, dx=1)
        up, down = step(over_win, own, dy=1), step(over_win, own, dy=-1)
        side_up, side_down = step(over_win, side, dy=1), step(over_win, side, dy=-1)
        far, side_far = step(over_win, up, dy=1), step(over_win, side_down, dy=-1)
        sources = [own, side, up, down, side_up, side_down, far, side_far]

        w = lax.axis_index("win")
        y, x = w // 2, w % 2
        order = jnp.stack([((y + dy) % 4) * 2 + (x + dx) % 2 for dy, dx in ring_order]).astype(jnp.int32)
        mine = slot_call(order, parts)
        side = step(over_chan, mine, dh=1)
        up, down = step(over_chan, mine, dz=1), step(over_chan, mine, dz=-1)
        side_up, side_down = step(over_chan, side, dz=1), step(over_chan, side, dz=-1)
        far, side_far = step(over_chan, up, dz=1), step(over_chan, side_down, dz=-1)
        pieces = [mine, side, up, down, side_up, side_down, far, side_far]
        pieces = pieces + [step(over_chan, r, dc=1) for r in pieces]
        ch = lax.axis_index("chan")
        z, h, c = ch // 4, (ch // 2) % 2, ch % 2
        places = [((z + dz) % 4) * 4 + ((h + dh) % 2) * 2 + (c + dc) % 2 for dc in range(2) for dz, dh in ring_order]

        out = None
        for take in ((0, 8, 1, 9, 2, 10, 3, 11), (4, 12, 5, 13, 6, 14, 7, 15)):
            at = jnp.stack([places[n] for n in take]).astype(jnp.int32)
            out = pair_call(at, sources, [pieces[n] for n in take], high, low, 16, out)
        return out

    return jax.shard_map(
        stages,
        mesh=mesh,
        in_specs=(P("win", "chan", None), P("win", "chan")),
        out_specs=P("chan", None, "win", None, None),
        check_vma=False,
    )
```

```python
import math

import jax
import jax.numpy as jnp
import numpy as np
from jax import lax
from jax.experimental import pallas as pl
from jax.experimental.pallas import tpu as pltpu
from jax.sharding import PartitionSpec as P

SAMPLES = 1500
BINS = 128
LAGS = 128
LOWEST = 6
ROWS = BINS + 1
CHUNK = 43
STEPS = ROWS // CHUNK
PITCH = 2 * BINS + 8
ROW = 24
SPAN = 512
PAIR_VMEM = 34 << 20
SPECTRA_VMEM = 67043328
SLOT_VMEM = 8 << 20


def build_tables():
    t = np.arange(SAMPLES)
    k = np.arange(BINS) + LOWEST
    angle = ((t[:, None] * k[None, :]) % SAMPLES).astype(np.float32) * np.float32(2.0 * math.pi / SAMPLES)
    hann = np.float32(0.5) - np.float32(0.5) * np.cos(t.astype(np.float32) * np.float32(2.0 * math.pi / SAMPLES))
    taper = np.concatenate([hann[:, None] * np.cos(angle), -hann[:, None] * np.sin(angle)], axis=1)
    taper = np.pad(taper.T, ((0, 0), (0, -SAMPLES % SPAN))).astype(jnp.bfloat16)
    j = np.arange(LAGS) - LAGS // 2
    lag_angle = ((k[:, None] * j[None, :]) % SAMPLES).astype(np.float32) * np.float32(2.0 * math.pi / SAMPLES)
    inverse = np.concatenate([np.cos(lag_angle), -np.sin(lag_angle)], axis=0)
    inverse = np.ascontiguousarray(inverse.T).astype(np.float32)
    high = inverse.astype(jnp.bfloat16)
    low = (inverse - high.astype(np.float32)).astype(jnp.bfloat16)
    return taper, high, low


def spectra_call(series, validity, taper):
    windows, channels, _ = series.shape
    slots = channels // 16
    groups = BINS // 8 + 1
    steps = taper.shape[1] // SPAN
    tail = SAMPLES - (steps - 1) * SPAN
    by_time = jnp.transpose(series, (2, 0, 1))

    def kernel(x_ref, v_ref, t_ref, w_ref, p_ref, turned, acc, scr):
        g = pl.program_id(0)

        def turn(q, _):
            block = x_ref[pl.ds(q * 4, 4)].astype(jnp.float32)
            for e in range(4):
                turned[pl.ds(q * 4 + e, windows, stride=SPAN + 8), :] = block[e]
            return 0

        @pl.when(g == 0)
        def _():
            acc[...] = jnp.zeros_like(acc)

        @pl.when(g < steps - 1)
        def _():
            lax.fori_loop(0, SPAN // 4, turn, 0, unroll=16)

        @pl.when(g == steps - 1)
        def _():
            lax.fori_loop(0, tail // 4, turn, 0, unroll=17)
            for q in range(tail, SPAN):
                turned[pl.ds(q, windows, stride=SPAN + 8), :] = jnp.zeros((windows, channels), jnp.float32)

        for h in range(windows // 2):
            cols = [turned[(2 * h + e) * (SPAN + 8) : (2 * h + e) * (SPAN + 8) + SPAN, :] for e in range(2)]
            cols = jnp.concatenate(cols, axis=1).astype(jnp.bfloat16)
            acc[h] += jnp.dot(t_ref[...], cols, preferred_element_type=jnp.float32)

        @pl.when(g == steps - 1)
        def _():
            for h in range(windows // 2):
                s = acc[h]
                energy = jnp.sum(s * s, axis=0, keepdims=True) * (1.0 / (2 * BINS))
                flags = v_ref[2 * h : 2 * h + 2, :].astype(jnp.float32)
                flags = jnp.concatenate([flags[0:1], flags[1:2]], axis=1)
                s = s * lax.rsqrt(energy + 1e-06) * flags
                for e in range(2):
                    for part in range(2):
                        scr[pl.ds(part * 8 + 2 * h + e, BINS, stride=16), :] = s[
                            part * BINS : (part + 1) * BINS, e * channels : (e + 1) * channels
                        ]
            for b in range(BINS // 8):
                block = scr[b * 128 : (b + 1) * 128, :]
                w_ref[b * 8 : (b + 1) * 8] = block.astype(jnp.bfloat16).reshape(8, 16, channels)
                p_ref[:, b] = block.T.astype(jnp.bfloat16).reshape(slots, 16, 128)
            f = v_ref[...].astype(jnp.float32)
            f = jnp.concatenate([f, jnp.zeros((8, channels), jnp.float32)], axis=0)
            w_ref[BINS] = f.astype(jnp.bfloat16)
            f = jnp.concatenate([f, jnp.zeros((112, channels), jnp.float32)], axis=0)
            p_ref[:, groups - 1] = f.T.astype(jnp.bfloat16).reshape(slots, 16, 128)

    return pl.pallas_call(
        kernel,
        grid=(steps,),
        in_specs=[
            pl.BlockSpec((SPAN, windows, channels), lambda g: (g, 0, 0)),
            pl.BlockSpec((windows, channels), lambda g: (0, 0)),
            pl.BlockSpec((2 * BINS, SPAN), lambda g: (0, g)),
        ],
        out_specs=[
            pl.BlockSpec((ROWS, 16, channels), lambda g: (0, 0, 0)),
            pl.BlockSpec((slots, groups, 16, 128), lambda g: (0, 0, 0, 0)),
        ],
        out_shape=[
            jax.ShapeDtypeStruct((ROWS, 16, channels), jnp.bfloat16),
            jax.ShapeDtypeStruct((slots, groups, 16, 128), jnp.bfloat16),
        ],
        scratch_shapes=[
            pltpu.VMEM((windows * (SPAN + 8), channels), jnp.float32),
            pltpu.VMEM((windows // 2, 2 * BINS, 2 * channels), jnp.float32),
            pltpu.VMEM((BINS * 16, channels), jnp.float32),
        ],
        compiler_params=pltpu.CompilerParams(dimension_semantics=("arbitrary",), vmem_limit_bytes=SPECTRA_VMEM),
        name="spectra",
    )(by_time, validity, taper)


def slot_call(order, parts):
    count, groups = parts.shape[:2]

    span = 9
    steps = pl.cdiv(groups, span)
    whole = groups - 1 - (steps - 1) * span

    def kernel(order_ref, p_ref, r_ref):
        g = pl.program_id(0)

        lane = lax.broadcasted_iota(jnp.int32, (16, 128), 1)

        def body(b, _):
            tiles = [p_ref[order_ref[q], b].astype(jnp.float32) for q in range(count)]
            for d in (4, 2, 1):
                low = (lane // (16 * d)) % 2 == 0
                for q in range(8):
                    if q & d == 0:
                        one, two = tiles[q], tiles[q + d]
                        tiles[q] = jnp.where(low, one, pltpu.roll(two, 16 * d, 1))
                        tiles[q + d] = jnp.where(low, pltpu.roll(one, 128 - 16 * d, 1), two)
            for e in range(8):
                r_ref[b * 8 + e] = tiles[e].astype(jnp.bfloat16)
            return 0

        @pl.when(g < steps - 1)
        def _():
            lax.fori_loop(0, span, body, 0, unroll=span)

        @pl.when(g == steps - 1)
        def _():
            lax.fori_loop(0, whole, body, 0, unroll=whole)
            r_ref[whole * 8] = jnp.concatenate([p_ref[order_ref[q], whole][:, :16] for q in range(count)], axis=1)

    return pl.pallas_call(
        kernel,
        grid_spec=pltpu.PrefetchScalarGridSpec(
            num_scalar_prefetch=1,
            grid=(steps,),
            in_specs=[pl.BlockSpec((count, span, 16, 128), lambda g, o: (0, g, 0, 0))],
            out_specs=pl.BlockSpec((span * 8, 16, 128), lambda g, o: (g, 0, 0)),
        ),
        out_shape=jax.ShapeDtypeStruct((ROWS, 16, 128), jnp.bfloat16),
        compiler_params=pltpu.CompilerParams(dimension_semantics=("arbitrary",), vmem_limit_bytes=SLOT_VMEM),
        name="slot",
    )(order, parts)


def pair_call(places, base, sources, receivers, high, low, blocks, previous=None):
    count = len(receivers)
    rows = 16 * count

    def kernel(place_ref, *refs):
        src = refs[:8]
        rcv = refs[8 : 8 + count]
        hi_ref, lo_ref = refs[8 + count : 10 + count]
        out, joined, recip, held, sent = refs[-5:]
        g = pl.program_id(0)

        def one_bin(k):
            tiles = [s[k] for s in src]
            swapped = []
            for tile in tiles:
                f = tile.astype(jnp.float32)
                swapped.append(jnp.concatenate([-f[8:], f[:8]], axis=0).astype(jnp.bfloat16))
            weights = jnp.concatenate([jnp.concatenate(tiles, axis=0), jnp.concatenate(swapped, axis=0)], axis=1)
            lhs = jnp.concatenate([r[k] for r in rcv], axis=0)
            return jnp.dot(lhs, weights, preferred_element_type=jnp.float32)

        def store_bin(k, _):
            both = one_bin(k)
            at = g * CHUNK + k
            joined[pl.ds(at, rows, stride=PITCH), :] = both[:, :128]
            joined[pl.ds(at + BINS, rows, stride=PITCH), :] = both[:, 128:]
            return 0

        @pl.when(g < STEPS)
        def _():
            lax.fori_loop(0, CHUNK - 1, store_bin, 0, unroll=42)

        @pl.when(g < STEPS - 1)
        def _():
            store_bin(CHUNK - 1, 0)

        @pl.when(g == STEPS - 1)
        def _():
            recip[...] = 1.0 / jnp.maximum(one_bin(CHUNK - 1)[:, :128], 1.0)

        @pl.when(g >= STEPS)
        def _():
            block = g - STEPS
            slot = lax.rem(block, 2)

            def write(which, at):
                return pltpu.make_async_copy(
                    held.at[at, :, pl.ds(0, 16), :], out.at[:, place_ref[base + which], 0], sent.at[at]
                )

            @pl.when(block >= 2)
            def _():
                write(block - 2, slot).wait()

            flat = held.at[slot].reshape(128 * ROW, LAGS)

            def body(q, _):
                i = (g - STEPS) * 16 + 2 * q
                first = pl.multiple_of(i * PITCH, 8)
                second = pl.multiple_of((i + 1) * PITCH, 8)
                pair = jnp.concatenate([joined[pl.ds(first, 256), :], joined[pl.ds(second, 256), :]], axis=1)
                upper = pair.astype(jnp.bfloat16)
                lower = (pair - upper.astype(jnp.float32)).astype(jnp.bfloat16)
                tables = jnp.concatenate([hi_ref[...], lo_ref[...]], axis=0)
                acc = jnp.dot(tables, upper, preferred_element_type=jnp.float32)
                acc = acc[:LAGS] + acc[LAGS:] + jnp.dot(hi_ref[...], lower, preferred_element_type=jnp.float32)
                scale = jnp.concatenate([recip[pl.ds(i, 1), :], recip[pl.ds(i + 1, 1), :]], axis=1)
                acc = acc * scale
                flat[pl.ds(2 * q, 128, stride=ROW), :] = acc[:, :128].T
                flat[pl.ds(2 * q + 1, 128, stride=ROW), :] = acc[:, 128:].T
                return 0

            lax.fori_loop(0, 8, body, 0, unroll=8)
            write(block, slot).start()

            @pl.when(block == count - 1)
            def _():
                write(block - 1, 1 - slot).wait()
                write(block, slot).wait()

    piece = pl.BlockSpec((CHUNK, 16, 128), lambda g, at: (jnp.minimum(g, STEPS - 1), 0, 0))
    table = pl.BlockSpec((LAGS, 2 * BINS), lambda g, at: (0, 0))
    in_specs = [piece] * (8 + count) + [table] * 2
    operands = [*sources, *receivers, high, low]
    aliases = {}
    if previous is not None:
        in_specs.append(pl.BlockSpec(memory_space=pl.ANY))
        aliases = {1 + len(operands): 0}
        operands.append(previous)
    macs = (ROWS * 128 * 256 + 128 * 128 * 256 * 3) * rows
    return pl.pallas_call(
        kernel,
        grid_spec=pltpu.PrefetchScalarGridSpec(
            num_scalar_prefetch=1,
            grid=(STEPS + count,),
            in_specs=in_specs,
            out_specs=pl.BlockSpec(memory_space=pl.ANY),
            scratch_shapes=[
                pltpu.VMEM((rows * PITCH, 128), jnp.float32),
                pltpu.VMEM((rows, 128), jnp.float32),
                pltpu.VMEM((2, 128, ROW, LAGS), jnp.float32),
                pltpu.SemaphoreType.DMA((2,)),
            ],
        ),
        out_shape=jax.ShapeDtypeStruct((128, blocks, 1, 16, LAGS), jnp.float32),
        input_output_aliases=aliases,
        compiler_params=pltpu.CompilerParams(dimension_semantics=("arbitrary",), vmem_limit_bytes=PAIR_VMEM),
        cost_estimate=pl.CostEstimate(flops=2 * macs, bytes_accessed=(8 + count) * ROWS * 4096, transcendentals=0),
    )(places, *operands)


def solution(mesh):
    taper, high, low = build_tables()

    def chan_of(z, h, c):
        return (z % 4) * 4 + (h % 2) * 2 + c % 2

    def win_of(y, x):
        return (y % 4) * 2 + x % 2

    def over_chan(a, dz=0, dh=0, dc=0):
        perm = [(chan_of(z, h, c), chan_of(z + dz, h + dh, c + dc)) for z in range(4) for h in range(2) for c in range(2)]
        return lax.ppermute(a, "chan", perm)

    def over_win(a, dy=0, dx=0):
        perm = [(win_of(y, x), win_of(y + dy, x + dx)) for y in range(4) for x in range(2)]
        return lax.ppermute(a, "win", perm)

    ring_order = ((0, 0), (0, 1), (-1, 0), (1, 0), (-1, 1), (1, 1), (-2, 0), (2, 1))

    def step(move, value, **by):
        return move(value, **by)

    def stages(series, validity):
        own, slots = spectra_call(series, validity, taper)

        parts = lax.all_to_all(slots, "win", split_axis=0, concat_axis=0, tiled=True)
        side = step(over_win, own, dx=1)
        up, down = step(over_win, own, dy=1), step(over_win, own, dy=-1)
        side_up, side_down = step(over_win, side, dy=1), step(over_win, side, dy=-1)
        far, side_far = step(over_win, up, dy=1), step(over_win, side_down, dy=-1)
        sources = [own, side, up, down, side_up, side_down, far, side_far]

        w = lax.axis_index("win")
        y, x = w // 2, w % 2
        ch = lax.axis_index("chan")
        z, h, c = ch // 4, (ch // 2) % 2, ch % 2
        order = [((y + dy) % 4) * 2 + (x + dx) % 2 for dy, dx in ring_order]
        blocks = [((z + dz) % 4) * 4 + ((h + dh) % 2) * 2 + (c + dc) % 2 for dc in range(2) for dz, dh in ring_order]
        first, second = (0, 8, 1, 9, 2, 10, 3, 11), (4, 12, 5, 13, 6, 14, 7, 15)
        where = jnp.stack(order + [blocks[n] for n in first + second]).astype(jnp.int32)
        mine = slot_call(where, parts)
        side = step(over_chan, mine, dh=1)
        up, down = step(over_chan, mine, dz=1), step(over_chan, mine, dz=-1)
        side_up, side_down = step(over_chan, side, dz=1), step(over_chan, side, dz=-1)
        far, side_far = step(over_chan, up, dz=1), step(over_chan, side_down, dz=-1)
        pieces = [mine, side, up, down, side_up, side_down, far, side_far]
        pieces = pieces + [step(over_chan, r, dc=1) for r in pieces]
        out = None
        for base, take in ((8, first), (16, second)):
            out = pair_call(where, base, sources, [pieces[n] for n in take], high, low, 16, out)
        return out

    return jax.shard_map(
        stages,
        mesh=mesh,
        in_specs=(P("win", "chan", None), P("win", "chan")),
        out_specs=P("chan", None, "win", None, None),
        check_vma=False,
    )
```

```python
import math

import jax
import jax.numpy as jnp
import numpy as np
from jax import lax
from jax.experimental import pallas as pl
from jax.experimental.pallas import tpu as pltpu
from jax.sharding import PartitionSpec as P

SAMPLES = 1500
BINS = 128
LAGS = 128
LOWEST = 6
ROWS = BINS + 1
CHUNK = 43
STEPS = ROWS // CHUNK
PITCH = 2 * BINS + 8
ROW = 24
SPAN = 512
PAIR_VMEM = 34 << 20
SPECTRA_VMEM = 67043328 - 1300000
SLOT_VMEM = 8 << 20


def build_tables():
    t = np.arange(SAMPLES)
    k = np.arange(BINS) + LOWEST
    angle = ((t[:, None] * k[None, :]) % SAMPLES).astype(np.float32) * np.float32(2.0 * math.pi / SAMPLES)
    hann = np.float32(0.5) - np.float32(0.5) * np.cos(t.astype(np.float32) * np.float32(2.0 * math.pi / SAMPLES))
    taper = np.concatenate([hann[:, None] * np.cos(angle), -hann[:, None] * np.sin(angle)], axis=1)
    taper = np.pad(taper.T, ((0, 0), (0, -SAMPLES % SPAN))).astype(jnp.bfloat16)
    j = np.arange(LAGS) - LAGS // 2
    lag_angle = ((k[:, None] * j[None, :]) % SAMPLES).astype(np.float32) * np.float32(2.0 * math.pi / SAMPLES)
    inverse = np.concatenate([np.cos(lag_angle), -np.sin(lag_angle)], axis=0)
    inverse = np.ascontiguousarray(inverse.T).astype(np.float32)
    high = inverse.astype(jnp.bfloat16)
    low = (inverse - high.astype(np.float32)).astype(jnp.bfloat16)
    return taper, np.concatenate([high, low], axis=0)


def spectra_call(series, validity, taper):
    windows, channels, _ = series.shape
    slots = channels // 16
    groups = BINS // 8 + 1
    steps = taper.shape[1] // SPAN
    tail = SAMPLES - (steps - 1) * SPAN
    by_time = jnp.transpose(series, (2, 0, 1))

    def kernel(x_ref, v_ref, t_ref, w_ref, p_ref, turned, acc, scr):
        g = pl.program_id(0)

        def turn(q, _):
            block = x_ref[pl.ds(q * 4, 4)].astype(jnp.float32)
            for e in range(4):
                turned[pl.ds(q * 4 + e, windows, stride=SPAN + 8), :] = block[e]
            return 0

        @pl.when(g == 0)
        def _():
            acc[...] = jnp.zeros_like(acc)

        @pl.when(g < steps - 1)
        def _():
            lax.fori_loop(0, SPAN // 4, turn, 0, unroll=16)

        @pl.when(g == steps - 1)
        def _():
            lax.fori_loop(0, tail // 4, turn, 0, unroll=17)
            for q in range(tail, SPAN):
                turned[pl.ds(q, windows, stride=SPAN + 8), :] = jnp.zeros((windows, channels), jnp.float32)

        for h in range(windows // 2):
            cols = [turned[(2 * h + e) * (SPAN + 8) : (2 * h + e) * (SPAN + 8) + SPAN, :] for e in range(2)]
            cols = jnp.concatenate(cols, axis=1).astype(jnp.bfloat16)
            acc[h] += jnp.dot(t_ref[...], cols, preferred_element_type=jnp.float32)

        @pl.when(g == steps - 1)
        def _():
            for h in range(windows // 2):
                s = acc[h]
                energy = jnp.sum(s * s, axis=0, keepdims=True) * (1.0 / (2 * BINS))
                flags = v_ref[2 * h : 2 * h + 2, :].astype(jnp.float32)
                flags = jnp.concatenate([flags[0:1], flags[1:2]], axis=1)
                s = s * lax.rsqrt(energy + 1e-06) * flags
                for e in range(2):
                    for part in range(2):
                        scr[pl.ds(part * 8 + 2 * h + e, BINS, stride=16), :] = s[
                            part * BINS : (part + 1) * BINS, e * channels : (e + 1) * channels
                        ]
            for b in range(BINS // 8):
                block = scr[b * 128 : (b + 1) * 128, :]
                w_ref[b * 8 : (b + 1) * 8] = block.astype(jnp.bfloat16).reshape(8, 16, channels)
                p_ref[:, b] = block.T.astype(jnp.bfloat16).reshape(slots, 16, 128)
            f = v_ref[...].astype(jnp.float32)
            f = jnp.concatenate([f, jnp.zeros((8, channels), jnp.float32)], axis=0)
            w_ref[BINS] = f.astype(jnp.bfloat16)
            f = jnp.concatenate([f, jnp.zeros((112, channels), jnp.float32)], axis=0)
            p_ref[:, groups - 1] = f.T.astype(jnp.bfloat16).reshape(slots, 16, 128)

    return pl.pallas_call(
        kernel,
        grid=(steps,),
        in_specs=[
            pl.BlockSpec((SPAN, windows, channels), lambda g: (g, 0, 0)),
            pl.BlockSpec((windows, channels), lambda g: (0, 0)),
            pl.BlockSpec((2 * BINS, SPAN), lambda g: (0, g)),
        ],
        out_specs=[
            pl.BlockSpec((ROWS, 16, channels), lambda g: (0, 0, 0)),
            pl.BlockSpec((slots, groups, 16, 128), lambda g: (0, 0, 0, 0)),
        ],
        out_shape=[
            jax.ShapeDtypeStruct((ROWS, 16, channels), jnp.bfloat16),
            jax.ShapeDtypeStruct((slots, groups, 16, 128), jnp.bfloat16),
        ],
        scratch_shapes=[
            pltpu.VMEM((windows * (SPAN + 8), channels), jnp.float32),
            pltpu.VMEM((windows // 2, 2 * BINS, 2 * channels), jnp.float32),
            pltpu.VMEM((BINS * 16, channels), jnp.float32),
        ],
        compiler_params=pltpu.CompilerParams(dimension_semantics=("arbitrary",), vmem_limit_bytes=SPECTRA_VMEM),
        name="spectra",
    )(by_time, validity, taper)


def slot_call(order, parts):
    count, groups = parts.shape[:2]

    span = 9
    steps = pl.cdiv(groups, span)
    whole = groups - 1 - (steps - 1) * span

    def kernel(order_ref, p_ref, r_ref):
        g = pl.program_id(0)

        lane = lax.broadcasted_iota(jnp.int32, (16, 128), 1)

        def body(b, _):
            tiles = [p_ref[order_ref[q], b].astype(jnp.float32) for q in range(count)]
            for d in (4, 2, 1):
                low = (lane // (16 * d)) % 2 == 0
                for q in range(8):
                    if q & d == 0:
                        one, two = tiles[q], tiles[q + d]
                        tiles[q] = jnp.where(low, one, pltpu.roll(two, 16 * d, 1))
                        tiles[q + d] = jnp.where(low, pltpu.roll(one, 128 - 16 * d, 1), two)
            for e in range(8):
                r_ref[b * 8 + e] = tiles[e].astype(jnp.bfloat16)
            return 0

        @pl.when(g < steps - 1)
        def _():
            lax.fori_loop(0, span, body, 0, unroll=span)

        @pl.when(g == steps - 1)
        def _():
            lax.fori_loop(0, whole, body, 0, unroll=whole)
            r_ref[whole * 8] = jnp.concatenate([p_ref[order_ref[q], whole][:, :16] for q in range(count)], axis=1)

    return pl.pallas_call(
        kernel,
        grid_spec=pltpu.PrefetchScalarGridSpec(
            num_scalar_prefetch=1,
            grid=(steps,),
            in_specs=[pl.BlockSpec((count, span, 16, 128), lambda g, o: (0, g, 0, 0))],
            out_specs=pl.BlockSpec((span * 8, 16, 128), lambda g, o: (g, 0, 0)),
        ),
        out_shape=jax.ShapeDtypeStruct((ROWS, 16, 128), jnp.bfloat16),
        compiler_params=pltpu.CompilerParams(dimension_semantics=("arbitrary",), vmem_limit_bytes=SLOT_VMEM),
        name="slot",
    )(order, parts)


def pair_call(places, base, sources, receivers, lags, blocks, previous=None):
    count = len(receivers)
    rows = 16 * count

    def kernel(place_ref, *refs):
        src = refs[:8]
        rcv = refs[8 : 8 + count]
        table_ref = refs[8 + count]
        out, joined, recip, held, tables, sent, fetched = refs[-7:]
        g = pl.program_id(0)

        fetch = pltpu.make_async_copy(table_ref, tables, fetched)

        @pl.when(g == 0)
        def _():
            fetch.start()

        @pl.when(g == STEPS)
        def _():
            fetch.wait()

        def one_bin(k):
            tiles = [s[k] for s in src]
            swapped = []
            for tile in tiles:
                f = tile.astype(jnp.float32)
                swapped.append(jnp.concatenate([-f[8:], f[:8]], axis=0).astype(jnp.bfloat16))
            weights = jnp.concatenate([jnp.concatenate(tiles, axis=0), jnp.concatenate(swapped, axis=0)], axis=1)
            lhs = jnp.concatenate([r[k] for r in rcv], axis=0)
            return jnp.dot(lhs, weights, preferred_element_type=jnp.float32)

        def store_bin(k, _):
            both = one_bin(k)
            at = g * CHUNK + k
            joined[pl.ds(at, rows, stride=PITCH), :] = both[:, :128]
            joined[pl.ds(at + BINS, rows, stride=PITCH), :] = both[:, 128:]
            return 0

        @pl.when(g < STEPS)
        def _():
            lax.fori_loop(0, CHUNK - 1, store_bin, 0, unroll=42)

        @pl.when(g < STEPS - 1)
        def _():
            store_bin(CHUNK - 1, 0)

        @pl.when(g == STEPS - 1)
        def _():
            recip[...] = 1.0 / jnp.maximum(one_bin(CHUNK - 1)[:, :128], 1.0)

        @pl.when(g >= STEPS)
        def _():
            block = g - STEPS
            slot = lax.rem(block, 2)

            def write(which, at):
                return pltpu.make_async_copy(
                    held.at[at, :, pl.ds(0, 16), :], out.at[:, place_ref[base + which], 0], sent.at[at]
                )

            @pl.when(block >= 2)
            def _():
                write(block - 2, slot).wait()

            flat = held.at[slot].reshape(128 * ROW, LAGS)

            def body(q, _):
                i = (g - STEPS) * 16 + 2 * q
                first = pl.multiple_of(i * PITCH, 8)
                second = pl.multiple_of((i + 1) * PITCH, 8)
                pair = jnp.concatenate([joined[pl.ds(first, 256), :], joined[pl.ds(second, 256), :]], axis=1)
                upper = pair.astype(jnp.bfloat16)
                lower = (pair - upper.astype(jnp.float32)).astype(jnp.bfloat16)
                acc = jnp.dot(tables[...], upper, preferred_element_type=jnp.float32)
                acc = acc[:LAGS] + acc[LAGS:] + jnp.dot(tables[:LAGS], lower, preferred_element_type=jnp.float32)
                scale = jnp.concatenate([recip[pl.ds(i, 1), :], recip[pl.ds(i + 1, 1), :]], axis=1)
                acc = acc * scale
                flat[pl.ds(2 * q, 128, stride=ROW), :] = acc[:, :128].T
                flat[pl.ds(2 * q + 1, 128, stride=ROW), :] = acc[:, 128:].T
                return 0

            lax.fori_loop(0, 8, body, 0, unroll=8)
            write(block, slot).start()

            @pl.when(block == count - 1)
            def _():
                write(block - 1, 1 - slot).wait()
                write(block, slot).wait()

    piece = pl.BlockSpec((CHUNK, 16, 128), lambda g, at: (jnp.minimum(g, STEPS - 1), 0, 0))
    in_specs = [piece] * (8 + count) + [pl.BlockSpec(memory_space=pltpu.HBM)]
    operands = [*sources, *receivers, lags]
    aliases = {}
    if previous is not None:
        in_specs.append(pl.BlockSpec(memory_space=pl.ANY))
        aliases = {1 + len(operands): 0}
        operands.append(previous)
    macs = (ROWS * 128 * 256 + 128 * 128 * 256 * 3) * rows
    return pl.pallas_call(
        kernel,
        grid_spec=pltpu.PrefetchScalarGridSpec(
            num_scalar_prefetch=1,
            grid=(STEPS + count,),
            in_specs=in_specs,
            out_specs=pl.BlockSpec(memory_space=pl.ANY),
            scratch_shapes=[
                pltpu.VMEM((rows * PITCH, 128), jnp.float32),
                pltpu.VMEM((rows, 128), jnp.float32),
                pltpu.VMEM((2, 128, ROW, LAGS), jnp.float32),
                pltpu.VMEM((2 * LAGS, 2 * BINS), jnp.bfloat16),
                pltpu.SemaphoreType.DMA((2,)),
                pltpu.SemaphoreType.DMA,
            ],
        ),
        out_shape=jax.ShapeDtypeStruct((128, blocks, 1, 16, LAGS), jnp.float32),
        input_output_aliases=aliases,
        compiler_params=pltpu.CompilerParams(dimension_semantics=("arbitrary",), vmem_limit_bytes=PAIR_VMEM),
        cost_estimate=pl.CostEstimate(flops=2 * macs, bytes_accessed=(8 + count) * ROWS * 4096, transcendentals=0),
    )(places, *operands)


def solution(mesh):
    taper, lags = build_tables()

    def chan_of(z, h, c):
        return (z % 4) * 4 + (h % 2) * 2 + c % 2

    def win_of(y, x):
        return (y % 4) * 2 + x % 2

    def over_chan(a, dz=0, dh=0, dc=0):
        perm = [(chan_of(z, h, c), chan_of(z + dz, h + dh, c + dc)) for z in range(4) for h in range(2) for c in range(2)]
        return lax.ppermute(a, "chan", perm)

    def over_win(a, dy=0, dx=0):
        perm = [(win_of(y, x), win_of(y + dy, x + dx)) for y in range(4) for x in range(2)]
        return lax.ppermute(a, "win", perm)

    ring_order = ((0, 0), (0, 1), (-1, 0), (1, 0), (-1, 1), (1, 1), (-2, 0), (2, 1))

    def step(move, value, **by):
        return move(value, **by)

    def stages(series, validity):
        own, slots = spectra_call(series, validity, taper)

        parts = lax.all_to_all(slots, "win", split_axis=0, concat_axis=0, tiled=True)
        side = step(over_win, own, dx=1)
        up, down = step(over_win, own, dy=1), step(over_win, own, dy=-1)
        side_up, side_down = step(over_win, side, dy=1), step(over_win, side, dy=-1)
        far, side_far = step(over_win, up, dy=1), step(over_win, side_down, dy=-1)
        sources = [own, side, up, down, side_up, side_down, far, side_far]

        w = lax.axis_index("win")
        y, x = w // 2, w % 2
        ch = lax.axis_index("chan")
        z, h, c = ch // 4, (ch // 2) % 2, ch % 2
        order = [((y + dy) % 4) * 2 + (x + dx) % 2 for dy, dx in ring_order]
        blocks = [((z + dz) % 4) * 4 + ((h + dh) % 2) * 2 + (c + dc) % 2 for dc in range(2) for dz, dh in ring_order]
        first, second = (0, 8, 1, 9, 2, 10, 3, 11), (4, 12, 5, 13, 6, 14, 7, 15)
        where = jnp.stack(order + [blocks[n] for n in first + second]).astype(jnp.int32)
        mine = slot_call(where, parts)
        side = step(over_chan, mine, dh=1)
        up, down = step(over_chan, mine, dz=1), step(over_chan, mine, dz=-1)
        side_up, side_down = step(over_chan, side, dz=1), step(over_chan, side, dz=-1)
        far, side_far = step(over_chan, up, dz=1), step(over_chan, side_down, dz=-1)
        pieces = [mine, side, up, down, side_up, side_down, far, side_far]
        pieces = pieces + [step(over_chan, r, dc=1) for r in pieces]
        out = None
        for base, take in ((8, first), (16, second)):
            out = pair_call(where, base, sources, [pieces[n] for n in take], lags, 16, out)
        return out

    return jax.shard_map(
        stages,
        mesh=mesh,
        in_specs=(P("win", "chan", None), P("win", "chan")),
        out_specs=P("chan", None, "win", None, None),
        check_vma=False,
    )
```
